32 devices in a mesh: groups: 2 (over y), ctx: 4 (over x, core), chan: 4 (over z).
Axes of the slice: x: 2, y: 2, z: 4, core: 2. Of those that a mesh axis runs over, the one named last changes fastest.
Arguments:
- stream: bfloat16 [1536, 4096], P(('groups', 'ctx'), 'chan'), parts along dimension 0, may hold values from -30 to 30
- in_weights: bfloat16 [2, 4096, 3, 2048], P(None, 'ctx', None, 'chan'), may hold values from -0.09375 to 0.09375
- out_weights: bfloat16 [2, 4096, 2048], P(None, 'ctx', 'chan'), may hold values from -0.125 to 0.125
- short_taps: bfloat16 [7, 2048], P(None, 'chan'), may hold values from -2.390625 to 2.390625
- medium_taps: bfloat16 [128, 128], P(None, 'chan'), may hold values from -0.5390625 to 0.5390625
- plan: int32 [4], replicated, may hold values from 0 to 1
Outputs:
- result: bfloat16 [1536, 4096], P(('groups', 'ctx'), 'chan'), parts along dimension 0
The draws below stay inside these ranges and needn't reach their ends.
There are 2 independent parts, one for each index of `groups`. The reference program is written for one: setup_inputs(seed, part) draws one part's arguments, and reference() takes and returns one part's arrays. A program takes and returns all parts, laid end to end along the dimension named above; an argument that names none is the same for every part. Nothing has to cross between parts.
All inputs are finite; a program needn't handle non-finite values.
Results may differ from the reference program's by a relative error of at most 0.03.
Values may be sent and summed in bfloat16 or wider, within the bound.
A program may use at most 128 MiB of HBM per device.

```python
import jax
import jax.numpy as jnp
from jax import lax

D = 4096
C = 2048
SHORT_TAPS = 7
MEDIUM_TAPS = 128
STEPS = 4
TOKENS = 768
GROUPS = 128
N_CHAN = 4


def draw_stream(key, part):
    key_list = jax.random.split(key, 4)
    row_scale = jnp.exp(jax.random.uniform(key_list[0], (TOKENS, 1), jnp.float32, jnp.log(0.3), jnp.log(3.0)))
    col_scale = jnp.exp(jax.random.uniform(key_list[1], (1, D), jnp.float32, jnp.log(0.3), jnp.log(3.0)))
    base_noise = jax.random.truncated_normal(key_list[3], -4.0, 4.0, (TOKENS, D), jnp.float32)
    return jnp.clip(base_noise * row_scale * col_scale, -30.0, 30.0).astype(jnp.bfloat16)


def with_ends(drawn, rng, low, high):
    place = [jax.random.randint(jax.random.fold_in(rng, axis), (), 0, length) for axis, length in enumerate(drawn.shape)]
    main_axis = drawn.shape.index(max(drawn.shape))
    beside = place[:main_axis] + [(place[main_axis] + 1) % drawn.shape[main_axis]] + place[main_axis + 1:]
    return drawn.at[tuple(place)].set(low).at[tuple(beside)].set(high)


def block_scale(stream_key, dims, shards, low, top_value):
    def one(dim, parts):
        heights = jax.random.uniform(jax.random.fold_in(jax.random.fold_in(stream_key, 6), dim), (parts,), jnp.float32, low / len(shards), top_value / len(shards))
        return jnp.repeat(jnp.exp(heights), dims[dim] // parts).reshape((-1,) + (1,) * (len(dims) - dim - 1))

    level = one(*shards[0])
    for cut in shards[1:]:
        level = level * one(*cut)
    return level


def bell_draw(key, extent, width, limit, pieces=(), kind=jnp.bfloat16):
    entries = jax.random.normal(key, extent, jnp.float32) * width
    if len(pieces) > 0:
        entries = block_scale(key, extent, pieces, -0.22, 0.18) * entries
    return jnp.clip(entries, min=-limit, max=limit).astype(kind)


def setup_inputs(seed: int = 0, part: int = 0) -> dict:
    seeds = jax.random.split(jax.random.key(seed), 7)
    own_keys = jax.random.split(jax.random.fold_in(seeds[6], part), 7)
    stream = draw_stream(jax.random.fold_in(jax.random.fold_in(seeds[6], part), 71), part)
    in_weights = bell_draw(seeds[1], (2, D, 3, C), D ** -0.5, 0.09375, ((1, 4), (3, 4)))
    out_weights = bell_draw(seeds[2], (2, D, C), C ** -0.5, 0.125, ((1, 4), (2, 4)))
    short_taps = bell_draw(seeds[3], (SHORT_TAPS, C), 0.4, 2.390625, ((1, 4),))
    medium_taps = bell_draw(seeds[4], (MEDIUM_TAPS, GROUPS), 0.09, 0.5390625, ((1, 4),))
    plan = with_ends(jax.random.randint(seeds[5], (STEPS,), 0, 2), jax.random.fold_in(seeds[5], 1), 0, 1).astype(jnp.int32)
    return {"stream": stream, "in_weights": in_weights, "out_weights": out_weights, "short_taps": short_taps, "medium_taps": medium_taps, "plan": plan}


def section_taps(section, short_taps, medium_taps):
    reach = medium_taps.shape[0]
    channels = short_taps.shape[1]
    padding = jnp.zeros((reach - short_taps.shape[0], channels), short_taps.dtype)
    short_full = jnp.concatenate([short_taps, padding], 0)
    group_size = channels // medium_taps.shape[1]
    medium_full = jnp.broadcast_to(medium_taps[:, :, None], (reach, medium_taps.shape[1], group_size)).reshape(reach, channels)
    return jnp.where(section == 0, short_full, medium_full)

def causal_filter(extended, filter_taps):
    reach = filter_taps.shape[0]
    length = extended.shape[0] - reach + 1
    taps_wide = filter_taps.astype(jnp.float32)

    def add_tap(tap_index, total):
        index_now = jnp.asarray(tap_index).astype(jnp.int32)
        start = (jnp.int32(reach - 1) - index_now).astype(jnp.int32)
        window = lax.dynamic_slice_in_dim(extended, start, length, 0).astype(jnp.float32)
        weight_row = lax.dynamic_index_in_dim(taps_wide, index_now, 0, keepdims=True)
        return total + weight_row * window
    start_total = jnp.zeros((length, extended.shape[1]), jnp.float32)
    return lax.fori_loop(0, reach, add_tap, start_total)

def reference(stream, in_weights, out_weights, short_taps, medium_taps, plan):
    hidden = stream
    tokens = stream.shape[0]
    block_width = C // N_CHAN
    for step_index in range(STEPS):
        section = plan[step_index]
        weight_in = lax.dynamic_index_in_dim(in_weights, section, 0, keepdims=False)
        weight_out = lax.dynamic_index_in_dim(out_weights, section, 0, keepdims=False)
        widened = hidden.astype(jnp.float32)
        row_scale = lax.rsqrt(lax.optimization_barrier(jnp.mean(widened * widened, axis=1, keepdims=True)) + 1e-05)
        projected = jnp.dot(hidden, weight_in.reshape(D, 3 * C), preferred_element_type=jnp.float32)
        projected = projected.reshape(tokens, 3, C) * row_scale[:, :, None]
        query_bf = projected[:, 0].astype(jnp.bfloat16)
        mixed_bf = (projected[:, 1] * projected[:, 2]).astype(jnp.bfloat16)
        history = jnp.zeros((MEDIUM_TAPS - 1, C), jnp.bfloat16)
        filtered = causal_filter(jnp.concatenate([history, mixed_bf], 0), section_taps(section, short_taps, medium_taps))
        gated_bf = (query_bf.astype(jnp.float32) * filtered).astype(jnp.bfloat16)
        update = jnp.zeros((tokens, D), jnp.float32)
        for block_index in range(N_CHAN):
            lower = block_index * block_width
            block_term = lax.dot_general(gated_bf[:, lower:lower + block_width], weight_out[:, lower:lower + block_width], (((1,), (1,)), ((), ())), preferred_element_type=jnp.float32)
            update = update + lax.optimization_barrier(block_term.astype(jnp.bfloat16)).astype(jnp.float32)
        hidden = (hidden.astype(jnp.float32) + update).astype(jnp.bfloat16)
    return hidden
```

```python
from functools import partial

import jax
import jax.numpy as jnp
from jax import lax
from jax.experimental import pallas as pl
from jax.experimental.pallas import tpu as pltpu
from jax.sharding import PartitionSpec as P

STEPS = 4


def passed_along(value, axis, steps):
    count = lax.axis_size(axis)
    leading, last = (max(0, -steps), min(count, count - steps))
    return lax.ppermute(value, axis, [(source, source + steps) for source in range(leading, last)])


def section_taps(section, short_taps, medium_taps):
    reach = medium_taps.shape[0]
    channels = short_taps.shape[1]
    padding = jnp.zeros((reach - short_taps.shape[0], channels), short_taps.dtype)
    short_full = jnp.concatenate([short_taps, padding], 0)
    group_size = channels // medium_taps.shape[1]
    medium_full = jnp.broadcast_to(
        medium_taps[:, :, None], (reach, medium_taps.shape[1], group_size)
    ).reshape(reach, channels)
    return jnp.where(section == 0, short_full, medium_full)


def causal_filter(extended, filter_taps):
    filtered = lax.conv_general_dilated(
        extended[None],
        filter_taps[::-1][:, None, :],
        (1,),
        "VALID",
        dimension_numbers=("NWC", "WIO", "NWC"),
        feature_group_count=filter_taps.shape[1],
        preferred_element_type=jnp.float32,
    )
    return filtered[0]


def filter_gate(projected, section, short_taps, medium_taps):
    query_bf = projected[:, 0].astype(jnp.bfloat16)
    mixed_bf = (projected[:, 1] * projected[:, 2]).astype(jnp.bfloat16)
    reach = medium_taps.shape[0]
    earlier = passed_along(mixed_bf[-reach:], "ctx", 1)
    extended = jnp.concatenate([earlier[1:], mixed_bf], 0)
    filtered = causal_filter(extended, section_taps(section, short_taps, medium_taps))
    return (query_bf.astype(jnp.float32) * filtered).astype(jnp.bfloat16)


def expand_rows(hidden):
    return lax.all_gather(hidden, "chan", axis=1, tiled=True)


def combine(hidden, partial_sum):
    update = lax.psum_scatter(
        partial_sum.astype(jnp.bfloat16), "chan", scatter_dimension=1, tiled=True
    ).astype(jnp.float32)
    return (hidden.astype(jnp.float32) + update).astype(jnp.bfloat16)


def advance(hidden, section, project, emit, short_taps, medium_taps):
    full_rows = expand_rows(hidden)
    widened = full_rows.astype(jnp.float32)
    row_scale = lax.rsqrt(jnp.mean(widened * widened, axis=1, keepdims=True) + 1e-05)
    projected, kept_in = project(full_rows, section)
    projected = projected.reshape(full_rows.shape[0], 3, -1) * row_scale[:, :, None]
    gated_bf = filter_gate(projected, section, short_taps, medium_taps)
    partial_sum, kept_out = emit(gated_bf, section)
    return (combine(hidden, partial_sum), kept_in, kept_out)


def stored_project(weights_in, full_rows, section):
    chosen = lax.dynamic_index_in_dim(weights_in, section, 0, keepdims=False)
    projected = jnp.dot(
        full_rows, chosen.reshape(chosen.shape[0], -1), preferred_element_type=jnp.float32
    )
    return (projected, weights_in)


def stored_emit(weights_out, gated_bf, section):
    chosen = lax.dynamic_index_in_dim(weights_out, section, 0, keepdims=False)
    product = lax.dot_general(
        gated_bf, chosen, (((1,), (1,)), ((), ())), preferred_element_type=jnp.float32
    )
    return (product, weights_out)


def shards(stream, in_weights, out_weights, short_taps, medium_taps, plan):
    hidden = stream
    weights_in, weights_out = (
        lax.all_gather(in_weights, "ctx", axis=1, tiled=True),
        lax.all_gather(out_weights, "ctx", axis=1, tiled=True),
    )
    first_step = 0
    for step_index in range(first_step, STEPS):
        hidden, weights_in, weights_out = advance(
            hidden,
            plan[step_index],
            partial(stored_project, weights_in),
            partial(stored_emit, weights_out),
            short_taps,
            medium_taps,
        )
    return hidden


CHUNKS = 6
PAD = 128
LANES = 128
BF = jnp.bfloat16
F32 = jnp.float32


def stationary_kernel(
    sizes, plan, stream, w_in, w_out, taps, out,
    h, p_send, p_recv, x_send, x_recv, own, ss_own, ss_recv, mixed, query, gat, acc, r_send, r_recv,
    init_s, init_r, ss_s, ss_r, p_s, p_r, x_s, x_r, g_s, g_r, r_s, r_r, b_s, b_r, o_s, o_r, local_sem,
):
    tokens, rows, block, width, half = sizes
    ctx, chan = lax.axis_index("ctx"), lax.axis_index("chan")
    n_ctx, n_chan = 4, 4
    side, core = ctx // 2, ctx % 2
    partner = {"ctx": side * 2 + (1 - core)}
    across = {"ctx": (1 - side) * 2 + core}
    diagonal = {"ctx": (1 - side) * 2 + (1 - core)}
    relations = (partner, across, diagonal)
    last = n_chan - 1
    place = (chan, last - chan)
    onward = ({"chan": jnp.minimum(chan + 1, last)}, {"chan": jnp.maximum(chan - 1, 0)})
    back = (onward[1], onward[0])

    def remote(source, target, send, recv, device):
        return pltpu.make_async_remote_copy(
            src_ref=source, dst_ref=target, send_sem=send, recv_sem=recv,
            device_id=device, device_id_type=pl.DeviceIdType.MESH,
        )

    barrier = pltpu.get_barrier_semaphore()
    for di in range(n_ctx):
        for dk in range(n_chan):
            if di or dk:
                pl.semaphore_signal(
                    barrier, inc=1,
                    device_id={"ctx": (ctx + di) % n_ctx, "chan": (chan + dk) % n_chan},
                    device_id_type=pl.DeviceIdType.MESH,
                )
    pl.semaphore_wait(barrier, n_ctx * n_chan - 1)

    block_rows = tokens // n_ctx
    mine = pl.ds(pl.multiple_of(ctx * block_rows, block_rows), block_rows)

    def init_copy(kappa):
        return remote(stream, h.at[mine, :], init_s.at[kappa], init_r.at[ctx], {"ctx": chan, "chan": kappa})

    def init_wait(source):
        there = pl.ds(source * block_rows, block_rows)
        return remote(stream, h.at[there, :], init_s.at[0], init_r.at[source], {"ctx": chan, "chan": 0})

    corner = ctx == chan
    for kappa in range(n_chan):
        @pl.when(jnp.logical_not(corner & (chan == kappa)))
        def _():
            init_copy(kappa).start()

    @pl.when(corner)
    def _():
        keep = pltpu.make_async_copy(stream, h.at[mine, :], local_sem)
        keep.start()
        keep.wait()

    mixed[pl.ds(0, PAD), :] = jnp.zeros((PAD, LANES), F32)
    for source in range(n_ctx):
        @pl.when(jnp.logical_not(corner & (ctx == source)))
        def _():
            init_wait(source).wait_recv()
    for kappa in range(n_chan):
        @pl.when(jnp.logical_not(corner & (chan == kappa)))
        def _():
            init_copy(kappa).wait_send()

    def span(t):
        return pl.ds(pl.multiple_of(t * rows, rows), rows)

    def ss_copy(rel, t):
        return remote(ss_own.at[t], ss_recv.at[rel, t], ss_s.at[rel, t], ss_r.at[rel, t], relations[rel])

    def p_copy(slot, t):
        return remote(p_send.at[slot, t], p_recv.at[slot, t], p_s.at[slot, t], p_r.at[slot, t], partner)

    def x_copy(t):
        return remote(x_send.at[t], x_recv.at[t], x_s.at[t], x_r.at[t], across)

    def lanes(index):
        return pl.ds(pl.multiple_of(index * LANES, LANES), LANES)

    def g_copy(kind, t, sending=True):
        owner = (1 - side) * 2 + core if kind == 2 else ctx
        if not sending:
            owner = (across["ctx"], partner["ctx"], diagonal["ctx"])[kind]
        ref = gat.at[span(t), lanes(owner)]
        return remote(ref, ref, g_s.at[kind, t], g_r.at[kind, t], across if kind == 0 else partner)

    def r_copy(d, t):
        return remote(r_send.at[d, t], r_recv.at[d, t], r_s.at[d, t], r_r.at[d, t], onward[d])

    def b_copy(d, t):
        ref = h.at[span(t), pl.ds(d * half, half)]
        return remote(ref, ref, b_s.at[d, t], b_r.at[d, t], back[d])

    def take_back(t):
        for d in range(2):
            @pl.when(place[d] < last)
            def _():
                b_copy(d, t).wait_recv()

            @pl.when((place[d] < last) & (place[d] > 0))
            def _():
                b_copy(d, t).start()

    def each(count, body):
        def wrapped(t, carry):
            body(t)
            return carry
        lax.fori_loop(0, count, wrapped, 0)

    def step(s, carry):
        section = plan[s]

        def project(t, index):
            return jnp.dot(h[span(t), :], w_in[section, index], preferred_element_type=F32)

        def enter(t):
            @pl.when(s > 0)
            def _():
                take_back(t)

            p_send[0, t] = project(t, diagonal["ctx"]).astype(BF)
            p_copy(0, t).start()
            wide = h[span(t), :].astype(F32)
            squares = (wide * wide).astype(BF)
            ss_own[t] = lax.dot_general(
                jnp.ones((8, squares.shape[1]), BF), squares, (((1,), (1,)), ((), ())), preferred_element_type=F32
            )
            for rel in range(3):
                ss_copy(rel, t).start()
            passing = project(t, across["ctx"])
            p_copy(0, t).wait_recv()
            x_send[t] = (passing + p_recv[0, t].astype(F32)).astype(BF)
            x_copy(t).start()
            p_send[1, t] = project(t, partner["ctx"]).astype(BF)
            p_copy(1, t).start()
            own[t] = project(t, ctx)

        each(CHUNKS, enter)

        def mix(t):
            for rel in range(3):
                ss_copy(rel, t).wait_recv()
            p_copy(1, t).wait_recv()
            x_copy(t).wait_recv()
            total = ss_own[t] + ss_recv[0, t] + ss_recv[1, t] + ss_recv[2, t]
            scale = lax.rsqrt(total * (1.0 / width) + 1e-05)
            scale = jnp.transpose(scale)[:, :1]
            parts = (own[t] + p_recv[1, t].astype(F32) + x_recv[t].astype(F32)) * scale
            query = parts[:, :LANES].astype(BF).astype(F32)
            product = parts[:, LANES:2 * LANES] * parts[:, 2 * LANES:]
            mixed[pl.ds(pl.multiple_of(PAD + t * rows, rows), rows), :] = product.astype(BF).astype(F32)

            def tap_block(jj, total):
                start = pl.multiple_of(PAD + t * rows - 8 * jj - 8, 8)
                window = mixed[pl.ds(start, rows + 8), :]
                weights = taps[section, jj]
                for c in range(8):
                    total = total + weights[c:c + 1, :] * window[8 - c:8 - c + rows, :]
                return total

            filtered = lax.fori_loop(0, taps.shape[1], tap_block, jnp.zeros((rows, LANES), F32))
            gat[span(t), lanes(ctx)] = (query * filtered).astype(BF)
            g_copy(0, t).start()
            g_copy(1, t).start()

        each(CHUNKS, mix)

        def emit(t):
            g_copy(0, t, False).wait_recv()
            g_copy(2, t).start()
            g_copy(1, t, False).wait_recv()

        each(CHUNKS, emit)

        def emit_dot(t):
            g_copy(2, t, False).wait_recv()
            gated = gat[span(t), :]
            for d in range(2):
                acc[d, t] = lax.dot_general(
                    gated, w_out[section, d], (((1,), (1,)), ((), ())), preferred_element_type=F32
                )

                @pl.when(place[d] == 0)
                def _():
                    r_send[d, t] = acc[d, t].astype(BF)
                    r_copy(d, t).start()

            @pl.when(s > 0)
            def _():
                for d in range(2):
                    @pl.when((place[d] < last) & (place[d] > 0))
                    def _():
                        b_copy(d, t).wait_send()

                    @pl.when(place[d] == last)
                    def _():
                        b_copy(d, t).wait_send()

        each(CHUNKS, emit_dot)

        def chain(u):
            for d in range(2):
                t = u - (place[d] - 1)
                inside = (t >= 0) & (t < CHUNKS)

                @pl.when(inside & (place[d] > 0) & (place[d] < last))
                def _():
                    r_copy(d, t).wait_recv()
                    r_send[d, t] = (acc[d, t] + r_recv[d, t].astype(F32)).astype(BF)
                    r_copy(d, t).start()

                @pl.when(inside & (place[d] == last))
                def _():
                    r_copy(d, t).wait_recv()
                    update = acc[d, t] + r_recv[d, t].astype(F32)
                    columns = pl.ds(d * half, half)
                    h[span(t), columns] = (h[span(t), columns].astype(F32) + update).astype(BF)
                    b_copy(d, t).start()

        each(CHUNKS + last - 1, chain)

        def settle(t):
            for slot in range(2):
                p_copy(slot, t).wait_send()
            for rel in range(3):
                ss_copy(rel, t).wait_send()
            x_copy(t).wait_send()
            for kind in range(3):
                g_copy(kind, t).wait_send()
            for d in range(2):
                @pl.when(place[d] < last)
                def _():
                    r_copy(d, t).wait_send()

        each(CHUNKS, settle)
        return carry

    lax.fori_loop(0, STEPS, step, 0)
    each(CHUNKS, take_back)

    def finish(t):
        for d in range(2):
            @pl.when(place[d] > 0)
            def _():
                b_copy(d, t).wait_send()

    each(CHUNKS, finish)

    def out_copy(target):
        there = pl.ds(target * block_rows, block_rows)
        return remote(h.at[there, :], out, o_s.at[target], o_r, {"ctx": target})

    @pl.when(corner)
    def _():
        for target in range(n_ctx):
            @pl.when(ctx != target)
            def _():
                out_copy(target).start()
        keep = pltpu.make_async_copy(h.at[mine, :], out, local_sem)
        keep.start()
        keep.wait()
        for target in range(n_ctx):
            @pl.when(ctx != target)
            def _():
                out_copy(target).wait_send()

    @pl.when(jnp.logical_not(corner))
    def _():
        out_copy(0).wait_recv()


def stationary(stream, in_weights, out_weights, short_taps, medium_taps, plan):
    n_ctx = lax.axis_size("ctx")
    n_chan = lax.axis_size("chan")
    ctx = lax.axis_index("ctx")
    features, channels = in_weights.shape[1], in_weights.shape[3]
    tokens = stream.shape[0] * n_ctx
    rows = tokens // CHUNKS
    half = features // 2
    block = 3 * LANES
    reach = medium_taps.shape[0]
    w_in = in_weights.reshape(2, features, 3, n_ctx, LANES).transpose(0, 3, 1, 2, 4).reshape(2, n_ctx, features, block)
    w_out = out_weights.reshape(2, 2, half, channels)
    taps = jnp.stack([section_taps(section, short_taps, medium_taps) for section in range(2)])
    taps = lax.dynamic_slice_in_dim(taps, ctx * LANES, LANES, 2).astype(F32)
    taps = taps.reshape(2, reach // 8, 8, LANES)
    vmem = pl.BlockSpec(memory_space=pltpu.VMEM)
    dma = pltpu.SemaphoreType.DMA
    scratch = [
        pltpu.VMEM((tokens, features), BF),
        pltpu.VMEM((2, CHUNKS, rows, block), BF),
        pltpu.VMEM((2, CHUNKS, rows, block), BF),
        pltpu.VMEM((CHUNKS, rows, block), BF),
        pltpu.VMEM((CHUNKS, rows, block), BF),
        pltpu.VMEM((CHUNKS, rows, block), F32),
        pltpu.VMEM((CHUNKS, 8, rows), F32),
        pltpu.VMEM((3, CHUNKS, 8, rows), F32),
        pltpu.VMEM((PAD + tokens, LANES), F32),
        pltpu.VMEM((8, LANES), F32),
        pltpu.VMEM((tokens, channels), BF),
        pltpu.VMEM((2, CHUNKS, rows, half), F32),
        pltpu.VMEM((2, CHUNKS, rows, half), BF),
        pltpu.VMEM((2, CHUNKS, rows, half), BF),
        dma((n_chan,)), dma((n_ctx,)),
        dma((3, CHUNKS)), dma((3, CHUNKS)),
        dma((2, CHUNKS)), dma((2, CHUNKS)),
        dma((CHUNKS,)), dma((CHUNKS,)),
        dma((3, CHUNKS)), dma((3, CHUNKS)),
        dma((2, CHUNKS)), dma((2, CHUNKS)),
        dma((2, CHUNKS)), dma((2, CHUNKS)),
        dma((n_ctx,)), dma(()), dma(()),
    ]
    sizes = (tokens, rows, block, features * n_ctx, half)
    return pl.pallas_call(
        partial(stationary_kernel, sizes),
        out_shape=jax.ShapeDtypeStruct(stream.shape, stream.dtype),
        in_specs=[pl.BlockSpec(memory_space=pltpu.SMEM)] + [vmem] * 4,
        out_specs=vmem,
        scratch_shapes=scratch,
        compiler_params=pltpu.CompilerParams(
            collective_id=0, has_side_effects=True, vmem_limit_bytes=60 * 1024 * 1024
        ),
    )(plan, stream, w_in, w_out, taps)


def fits(mesh, stream, in_weights, medium_taps):
    n_ctx, n_chan = mesh.shape["ctx"], mesh.shape["chan"]
    tokens = stream.shape[0] // mesh.shape["groups"]
    channels = in_weights.shape[3] // n_chan
    return (
        n_ctx == 4 and n_chan == 4 and channels == n_ctx * LANES
        and stream.shape[1] // n_chan == in_weights.shape[1] // n_ctx
        and tokens % (CHUNKS * PAD) == 0 and medium_taps.shape[0] <= PAD and tokens // CHUNKS == PAD
    )


def solution(mesh):
    def run(stream, in_weights, out_weights, short_taps, medium_taps, plan):
        body = stationary if fits(mesh, stream, in_weights, medium_taps) else shards
        return jax.shard_map(
            body,
            mesh=mesh,
            in_specs=(
                P(("groups", "ctx"), "chan"),
                P(None, "ctx", None, "chan"),
                P(None, "ctx", "chan"),
                P(None, "chan"),
                P(None, "chan"),
                P(),
            ),
            out_specs=P(("groups", "ctx"), "chan"),
            check_vma=False,
        )(stream, in_weights, out_weights, short_taps, medium_taps, plan)

    return run
```

```python
from functools import partial

import jax
import jax.numpy as jnp
from jax import lax
from jax.experimental import pallas as pl
from jax.experimental.pallas import tpu as pltpu
from jax.sharding import PartitionSpec as P

STEPS = 4


def passed_along(value, axis, steps):
    count = lax.axis_size(axis)
    leading, last = (max(0, -steps), min(count, count - steps))
    return lax.ppermute(value, axis, [(source, source + steps) for source in range(leading, last)])


def section_taps(section, short_taps, medium_taps):
    reach = medium_taps.shape[0]
    channels = short_taps.shape[1]
    padding = jnp.zeros((reach - short_taps.shape[0], channels), short_taps.dtype)
    short_full = jnp.concatenate([short_taps, padding], 0)
    group_size = channels // medium_taps.shape[1]
    medium_full = jnp.broadcast_to(
        medium_taps[:, :, None], (reach, medium_taps.shape[1], group_size)
    ).reshape(reach, channels)
    return jnp.where(section == 0, short_full, medium_full)


def causal_filter(extended, filter_taps):
    filtered = lax.conv_general_dilated(
        extended[None],
        filter_taps[::-1][:, None, :],
        (1,),
        "VALID",
        dimension_numbers=("NWC", "WIO", "NWC"),
        feature_group_count=filter_taps.shape[1],
        preferred_element_type=jnp.float32,
    )
    return filtered[0]


def filter_gate(projected, section, short_taps, medium_taps):
    query_bf = projected[:, 0].astype(jnp.bfloat16)
    mixed_bf = (projected[:, 1] * projected[:, 2]).astype(jnp.bfloat16)
    reach = medium_taps.shape[0]
    earlier = passed_along(mixed_bf[-reach:], "ctx", 1)
    extended = jnp.concatenate([earlier[1:], mixed_bf], 0)
    filtered = causal_filter(extended, section_taps(section, short_taps, medium_taps))
    return (query_bf.astype(jnp.float32) * filtered).astype(jnp.bfloat16)


def expand_rows(hidden):
    return lax.all_gather(hidden, "chan", axis=1, tiled=True)


def combine(hidden, partial_sum):
    update = lax.psum_scatter(
        partial_sum.astype(jnp.bfloat16), "chan", scatter_dimension=1, tiled=True
    ).astype(jnp.float32)
    return (hidden.astype(jnp.float32) + update).astype(jnp.bfloat16)


def advance(hidden, section, project, emit, short_taps, medium_taps):
    full_rows = expand_rows(hidden)
    widened = full_rows.astype(jnp.float32)
    row_scale = lax.rsqrt(jnp.mean(widened * widened, axis=1, keepdims=True) + 1e-05)
    projected, kept_in = project(full_rows, section)
    projected = projected.reshape(full_rows.shape[0], 3, -1) * row_scale[:, :, None]
    gated_bf = filter_gate(projected, section, short_taps, medium_taps)
    partial_sum, kept_out = emit(gated_bf, section)
    return (combine(hidden, partial_sum), kept_in, kept_out)


def stored_project(weights_in, full_rows, section):
    chosen = lax.dynamic_index_in_dim(weights_in, section, 0, keepdims=False)
    projected = jnp.dot(
        full_rows, chosen.reshape(chosen.shape[0], -1), preferred_element_type=jnp.float32
    )
    return (projected, weights_in)


def stored_emit(weights_out, gated_bf, section):
    chosen = lax.dynamic_index_in_dim(weights_out, section, 0, keepdims=False)
    product = lax.dot_general(
        gated_bf, chosen, (((1,), (1,)), ((), ())), preferred_element_type=jnp.float32
    )
    return (product, weights_out)


def shards(stream, in_weights, out_weights, short_taps, medium_taps, plan):
    hidden = stream
    weights_in, weights_out = (
        lax.all_gather(in_weights, "ctx", axis=1, tiled=True),
        lax.all_gather(out_weights, "ctx", axis=1, tiled=True),
    )
    first_step = 0
    for step_index in range(first_step, STEPS):
        hidden, weights_in, weights_out = advance(
            hidden,
            plan[step_index],
            partial(stored_project, weights_in),
            partial(stored_emit, weights_out),
            short_taps,
            medium_taps,
        )
    return hidden


CHUNKS = 6
SKEW = 2
PAD = 128
LANES = 128
BF = jnp.bfloat16
F32 = jnp.float32


def stationary_kernel(
    sizes, plan, stream, w_in, w_out, taps, out,
    h, p_send, p_recv, x_send, x_recv, own, ss_own, ss_recv, mixed, query, gat, acc, r_send, r_recv,
    init_s, init_r, ss_s, ss_r, p_s, p_r, x_s, x_r, g_s, g_r, r_s, r_r, b_s, b_r, o_s, o_r, local_sem,
):
    tokens, rows, block, width, half = sizes
    ctx, chan = lax.axis_index("ctx"), lax.axis_index("chan")
    n_ctx, n_chan = 4, 4
    side, core = ctx // 2, ctx % 2
    partner = {"ctx": side * 2 + (1 - core)}
    across = {"ctx": (1 - side) * 2 + core}
    diagonal = {"ctx": (1 - side) * 2 + (1 - core)}
    relations = (partner, across, diagonal)
    last = n_chan - 1
    place = (chan, last - chan)
    onward = ({"chan": jnp.minimum(chan + 1, last)}, {"chan": jnp.maximum(chan - 1, 0)})
    back = (onward[1], onward[0])

    def remote(source, target, send, recv, device):
        return pltpu.make_async_remote_copy(
            src_ref=source, dst_ref=target, send_sem=send, recv_sem=recv,
            device_id=device, device_id_type=pl.DeviceIdType.MESH,
        )

    barrier = pltpu.get_barrier_semaphore()
    for di in range(n_ctx):
        for dk in range(n_chan):
            if di or dk:
                pl.semaphore_signal(
                    barrier, inc=1,
                    device_id={"ctx": (ctx + di) % n_ctx, "chan": (chan + dk) % n_chan},
                    device_id_type=pl.DeviceIdType.MESH,
                )
    pl.semaphore_wait(barrier, n_ctx * n_chan - 1)

    block_rows = tokens // n_ctx
    mine = pl.ds(pl.multiple_of(ctx * block_rows, block_rows), block_rows)

    def init_copy(kappa):
        return remote(stream, h.at[mine, :], init_s.at[kappa], init_r.at[ctx], {"ctx": chan, "chan": kappa})

    def init_wait(source):
        there = pl.ds(source * block_rows, block_rows)
        return remote(stream, h.at[there, :], init_s.at[0], init_r.at[source], {"ctx": chan, "chan": 0})

    corner = ctx == chan
    for kappa in range(n_chan):
        @pl.when(jnp.logical_not(corner & (chan == kappa)))
        def _():
            init_copy(kappa).start()

    @pl.when(corner)
    def _():
        keep = pltpu.make_async_copy(stream, h.at[mine, :], local_sem)
        keep.start()
        keep.wait()

    mixed[pl.ds(0, PAD), :] = jnp.zeros((PAD, LANES), F32)
    for source in range(n_ctx):
        @pl.when(jnp.logical_not(corner & (ctx == source)))
        def _():
            init_wait(source).wait_recv()
    for kappa in range(n_chan):
        @pl.when(jnp.logical_not(corner & (chan == kappa)))
        def _():
            init_copy(kappa).wait_send()

    def span(t):
        return pl.ds(pl.multiple_of(t * rows, rows), rows)

    def ss_copy(rel, t):
        return remote(ss_own.at[t], ss_recv.at[rel, t], ss_s.at[rel, t], ss_r.at[rel, t], relations[rel])

    def p_copy(slot, t):
        return remote(p_send.at[slot, t], p_recv.at[slot, t], p_s.at[slot, t], p_r.at[slot, t], partner)

    def x_copy(t):
        return remote(x_send.at[t], x_recv.at[t], x_s.at[t], x_r.at[t], across)

    def lanes(index):
        return pl.ds(pl.multiple_of(index * LANES, LANES), LANES)

    def g_copy(kind, t, sending=True):
        owner = (1 - side) * 2 + core if kind == 2 else ctx
        if not sending:
            owner = (across["ctx"], partner["ctx"], diagonal["ctx"])[kind]
        ref = gat.at[span(t), lanes(owner)]
        return remote(ref, ref, g_s.at[kind, t], g_r.at[kind, t], across if kind == 0 else partner)

    def r_copy(d, t):
        return remote(r_send.at[d, t], r_recv.at[d, t], r_s.at[d, t], r_r.at[d, t], onward[d])

    def b_copy(d, t):
        ref = h.at[span(t), pl.ds(d * half, half)]
        return remote(ref, ref, b_s.at[d, t], b_r.at[d, t], back[d])

    def arrive(t):
        for d in range(2):
            @pl.when(place[d] == 0)
            def _():
                b_copy(d, t).wait_recv()

    def each(count, body):
        def wrapped(t, carry):
            body(t)
            return carry
        lax.fori_loop(0, count, wrapped, 0)

    def step(s, carry):
        section = plan[s]

        def project(t, index):
            columns = lanes(index)
            weights = jnp.concatenate([w_in[section, j, :, columns] for j in range(3)], 1)
            return jnp.dot(h[span(t), :], weights, preferred_element_type=F32)

        def enter(t):
            p_send[0, t] = project(t, diagonal["ctx"]).astype(BF)
            p_copy(0, t).start()
            p_send[1, t] = project(t, partner["ctx"]).astype(BF)
            p_copy(1, t).start()
            wide = h[span(t), :].astype(F32)
            squares = (wide * wide).astype(BF)
            ss_own[t] = lax.dot_general(
                jnp.ones((8, squares.shape[1]), BF), squares, (((1,), (1,)), ((), ())), preferred_element_type=F32
            )
            for rel in range(3):
                ss_copy(rel, t).start()

        def cross(t):
            passing = project(t, across["ctx"])
            p_copy(0, t).wait_recv()
            x_send[t] = (passing + p_recv[0, t].astype(F32)).astype(BF)
            x_copy(t).start()
            own[t] = project(t, ctx)

        def entering(u):
            @pl.when(u < CHUNKS)
            def _():
                @pl.when(s > 0)
                def _():
                    arrive(u)

                enter(u)

            @pl.when(u > 0)
            def _():
                cross(u - 1)

        each(CHUNKS + 1, entering)

        def mix(t):
            for rel in range(3):
                ss_copy(rel, t).wait_recv()
            p_copy(1, t).wait_recv()
            x_copy(t).wait_recv()
            total = ss_own[t] + ss_recv[0, t] + ss_recv[1, t] + ss_recv[2, t]
            scale = lax.rsqrt(total * (1.0 / width) + 1e-05)
            scale = jnp.transpose(scale)[:, :1]
            parts = (own[t] + p_recv[1, t].astype(F32) + x_recv[t].astype(F32)) * scale
            query = parts[:, :LANES].astype(BF).astype(F32)
            product = parts[:, LANES:2 * LANES] * parts[:, 2 * LANES:]
            mixed[pl.ds(pl.multiple_of(PAD + t * rows, rows), rows), :] = product.astype(BF).astype(F32)

            def tap_block(jj, total):
                start = pl.multiple_of(PAD + t * rows - 8 * jj - 8, 8)
                window = mixed[pl.ds(start, rows + 8), :]
                weights = taps[section, jj]
                for c in range(8):
                    total = total + weights[c:c + 1, :] * window[8 - c:8 - c + rows, :]
                return total

            filtered = lax.fori_loop(0, taps.shape[1], tap_block, jnp.zeros((rows, LANES), F32))
            gat[span(t), lanes(ctx)] = (query * filtered).astype(BF)
            g_copy(0, t).start()
            g_copy(1, t).start()

        each(CHUNKS, mix)

        def emit(t):
            g_copy(0, t, False).wait_recv()
            g_copy(2, t).start()
            g_copy(1, t, False).wait_recv()

        each(CHUNKS, emit)

        def emit_dot(t):
            g_copy(2, t, False).wait_recv()
            gated = gat[span(t), :]
            for d in range(2):
                acc[d, t] = lax.dot_general(
                    gated, w_out[section, d], (((1,), (1,)), ((), ())), preferred_element_type=F32
                )

                @pl.when(place[d] == 0)
                def _():
                    r_send[d, t] = acc[d, t].astype(BF)
                    r_copy(d, t).start()

            @pl.when(s > 0)
            def _():
                for d in range(2):
                    @pl.when((place[d] < last) & (place[d] > 0))
                    def _():
                        b_copy(d, t).wait_send()

                    @pl.when(place[d] == last)
                    def _():
                        b_copy(d, t).wait_send()

        each(CHUNKS, emit_dot)

        def chain(u):
            for d in range(2):
                t = u - (place[d] - 1) * SKEW
                inside = (t >= 0) & (t < CHUNKS)

                @pl.when(inside & (place[d] > 0) & (place[d] < last))
                def _():
                    r_copy(d, t).wait_recv()
                    r_send[d, t] = (acc[d, t] + r_recv[d, t].astype(F32)).astype(BF)
                    r_copy(d, t).start()

                @pl.when(inside & (place[d] == last))
                def _():
                    r_copy(d, t).wait_recv()
                    update = acc[d, t] + r_recv[d, t].astype(F32)
                    columns = pl.ds(d * half, half)
                    h[span(t), columns] = (h[span(t), columns].astype(F32) + update).astype(BF)
                    b_copy(d, t).start()

            for d in range(2):
                t = u - (2 + last - place[d]) * SKEW
                inside = (t >= 0) & (t < CHUNKS)

                @pl.when(inside & (place[d] > 0) & (place[d] < last))
                def _():
                    b_copy(d, t).wait_recv()
                    b_copy(d, t).start()

        each(CHUNKS + (2 * last - 2) * SKEW, chain)

        def settle(t):
            for slot in range(2):
                p_copy(slot, t).wait_send()
            for rel in range(3):
                ss_copy(rel, t).wait_send()
            x_copy(t).wait_send()
            for kind in range(3):
                g_copy(kind, t).wait_send()
            for d in range(2):
                @pl.when(place[d] < last)
                def _():
                    r_copy(d, t).wait_send()

        each(CHUNKS, settle)
        return carry

    lax.fori_loop(0, STEPS, step, 0)
    each(CHUNKS, arrive)

    def finish(t):
        for d in range(2):
            @pl.when(place[d] > 0)
            def _():
                b_copy(d, t).wait_send()

    each(CHUNKS, finish)

    def out_copy(target):
        there = pl.ds(target * block_rows, block_rows)
        return remote(h.at[there, :], out, o_s.at[target], o_r, {"ctx": target})

    @pl.when(corner)
    def _():
        for target in range(n_ctx):
            @pl.when(ctx != target)
            def _():
                out_copy(target).start()
        keep = pltpu.make_async_copy(h.at[mine, :], out, local_sem)
        keep.start()
        keep.wait()
        for target in range(n_ctx):
            @pl.when(ctx != target)
            def _():
                out_copy(target).wait_send()

    @pl.when(jnp.logical_not(corner))
    def _():
        out_copy(0).wait_recv()


def stationary(stream, in_weights, out_weights, short_taps, medium_taps, plan):
    n_ctx = lax.axis_size("ctx")
    n_chan = lax.axis_size("chan")
    ctx = lax.axis_index("ctx")
    features, channels = in_weights.shape[1], in_weights.shape[3]
    tokens = stream.shape[0] * n_ctx
    rows = tokens // CHUNKS
    half = features // 2
    block = 3 * LANES
    reach = medium_taps.shape[0]
    w_in = in_weights.transpose(0, 2, 1, 3)
    w_out = out_weights.reshape(2, 2, half, channels)
    taps = jnp.stack([section_taps(section, short_taps, medium_taps) for section in range(2)])
    taps = lax.dynamic_slice_in_dim(taps, ctx * LANES, LANES, 2).astype(F32)
    taps = taps.reshape(2, reach // 8, 8, LANES)
    vmem = pl.BlockSpec(memory_space=pltpu.VMEM)
    dma = pltpu.SemaphoreType.DMA
    scratch = [
        pltpu.VMEM((tokens, features), BF),
        pltpu.VMEM((2, CHUNKS, rows, block), BF),
        pltpu.VMEM((2, CHUNKS, rows, block), BF),
        pltpu.VMEM((CHUNKS, rows, block), BF),
        pltpu.VMEM((CHUNKS, rows, block), BF),
        pltpu.VMEM((CHUNKS, rows, block), F32),
        pltpu.VMEM((CHUNKS, 8, rows), F32),
        pltpu.VMEM((3, CHUNKS, 8, rows), F32),
        pltpu.VMEM((PAD + tokens, LANES), F32),
        pltpu.VMEM((8, LANES), F32),
        pltpu.VMEM((tokens, channels), BF),
        pltpu.VMEM((2, CHUNKS, rows, half), F32),
        pltpu.VMEM((2, CHUNKS, rows, half), BF),
        pltpu.VMEM((2, CHUNKS, rows, half), BF),
        dma((n_chan,)), dma((n_ctx,)),
        dma((3, CHUNKS)), dma((3, CHUNKS)),
        dma((2, CHUNKS)), dma((2, CHUNKS)),
        dma((CHUNKS,)), dma((CHUNKS,)),
        dma((3, CHUNKS)), dma((3, CHUNKS)),
        dma((2, CHUNKS)), dma((2, CHUNKS)),
        dma((2, CHUNKS)), dma((2, CHUNKS)),
        dma((n_ctx,)), dma(()), dma(()),
    ]
    sizes = (tokens, rows, block, features * n_ctx, half)
    return pl.pallas_call(
        partial(stationary_kernel, sizes),
        out_shape=jax.ShapeDtypeStruct(stream.shape, stream.dtype),
        in_specs=[pl.BlockSpec(memory_space=pltpu.SMEM)] + [vmem] * 4,
        out_specs=vmem,
        scratch_shapes=scratch,
        compiler_params=pltpu.CompilerParams(
            collective_id=0, has_side_effects=True, vmem_limit_bytes=60 * 1024 * 1024
        ),
    )(plan, stream, w_in, w_out, taps)


def fits(mesh, stream, in_weights, medium_taps):
    n_ctx, n_chan = mesh.shape["ctx"], mesh.shape["chan"]
    tokens = stream.shape[0] // mesh.shape["groups"]
    channels = in_weights.shape[3] // n_chan
    return (
        n_ctx == 4 and n_chan == 4 and channels == n_ctx * LANES
        and stream.shape[1] // n_chan == in_weights.shape[1] // n_ctx
        and tokens % (CHUNKS * PAD) == 0 and medium_taps.shape[0] <= PAD
    )


def solution(mesh):
    def run(stream, in_weights, out_weights, short_taps, medium_taps, plan):
        body = stationary if fits(mesh, stream, in_weights, medium_taps) else shards
        return jax.shard_map(
            body,
            mesh=mesh,
            in_specs=(
                P(("groups", "ctx"), "chan"),
                P(None, "ctx", None, "chan"),
                P(None, "ctx", "chan"),
                P(None, "chan"),
                P(None, "chan"),
                P(),
            ),
            out_specs=P(("groups", "ctx"), "chan"),
            check_vma=False,
        )(stream, in_weights, out_weights, short_taps, medium_taps, plan)

    return run
```

```python
from functools import partial

import jax
import jax.numpy as jnp
from jax import lax
from jax.experimental import pallas as pl
from jax.experimental.pallas import tpu as pltpu
from jax.sharding import PartitionSpec as P

STEPS = 4


def passed_along(value, axis, steps):
    count = lax.axis_size(axis)
    leading, last = (max(0, -steps), min(count, count - steps))
    return lax.ppermute(value, axis, [(source, source + steps) for source in range(leading, last)])


def section_taps(section, short_taps, medium_taps):
    reach = medium_taps.shape[0]
    channels = short_taps.shape[1]
    padding = jnp.zeros((reach - short_taps.shape[0], channels), short_taps.dtype)
    short_full = jnp.concatenate([short_taps, padding], 0)
    group_size = channels // medium_taps.shape[1]
    medium_full = jnp.broadcast_to(
        medium_taps[:, :, None], (reach, medium_taps.shape[1], group_size)
    ).reshape(reach, channels)
    return jnp.where(section == 0, short_full, medium_full)


def causal_filter(extended, filter_taps):
    filtered = lax.conv_general_dilated(
        extended[None],
        filter_taps[::-1][:, None, :],
        (1,),
        "VALID",
        dimension_numbers=("NWC", "WIO", "NWC"),
        feature_group_count=filter_taps.shape[1],
        preferred_element_type=jnp.float32,
    )
    return filtered[0]


def filter_gate(projected, section, short_taps, medium_taps):
    query_bf = projected[:, 0].astype(jnp.bfloat16)
    mixed_bf = (projected[:, 1] * projected[:, 2]).astype(jnp.bfloat16)
    reach = medium_taps.shape[0]
    earlier = passed_along(mixed_bf[-reach:], "ctx", 1)
    extended = jnp.concatenate([earlier[1:], mixed_bf], 0)
    filtered = causal_filter(extended, section_taps(section, short_taps, medium_taps))
    return (query_bf.astype(jnp.float32) * filtered).astype(jnp.bfloat16)


def expand_rows(hidden):
    return lax.all_gather(hidden, "chan", axis=1, tiled=True)


def combine(hidden, partial_sum):
    update = lax.psum_scatter(
        partial_sum.astype(jnp.bfloat16), "chan", scatter_dimension=1, tiled=True
    ).astype(jnp.float32)
    return (hidden.astype(jnp.float32) + update).astype(jnp.bfloat16)


def advance(hidden, section, project, emit, short_taps, medium_taps):
    full_rows = expand_rows(hidden)
    widened = full_rows.astype(jnp.float32)
    row_scale = lax.rsqrt(jnp.mean(widened * widened, axis=1, keepdims=True) + 1e-05)
    projected, kept_in = project(full_rows, section)
    projected = projected.reshape(full_rows.shape[0], 3, -1) * row_scale[:, :, None]
    gated_bf = filter_gate(projected, section, short_taps, medium_taps)
    partial_sum, kept_out = emit(gated_bf, section)
    return (combine(hidden, partial_sum), kept_in, kept_out)


def stored_project(weights_in, full_rows, section):
    chosen = lax.dynamic_index_in_dim(weights_in, section, 0, keepdims=False)
    projected = jnp.dot(
        full_rows, chosen.reshape(chosen.shape[0], -1), preferred_element_type=jnp.float32
    )
    return (projected, weights_in)


def stored_emit(weights_out, gated_bf, section):
    chosen = lax.dynamic_index_in_dim(weights_out, section, 0, keepdims=False)
    product = lax.dot_general(
        gated_bf, chosen, (((1,), (1,)), ((), ())), preferred_element_type=jnp.float32
    )
    return (product, weights_out)


def shards(stream, in_weights, out_weights, short_taps, medium_taps, plan):
    hidden = stream
    weights_in, weights_out = (
        lax.all_gather(in_weights, "ctx", axis=1, tiled=True),
        lax.all_gather(out_weights, "ctx", axis=1, tiled=True),
    )
    first_step = 0
    for step_index in range(first_step, STEPS):
        hidden, weights_in, weights_out = advance(
            hidden,
            plan[step_index],
            partial(stored_project, weights_in),
            partial(stored_emit, weights_out),
            short_taps,
            medium_taps,
        )
    return hidden


CHUNKS = 6
SKEW = 2
ENTRY = 9
PAD = 128
LANES = 128
BF = jnp.bfloat16
F32 = jnp.float32


def stationary_kernel(
    sizes, plan, stream, w_in, w_out, taps, out,
    h, p_send, p_recv, x_send, x_recv, own, ss_own, ss_recv, mixed, query, gat, acc, r_send, r_recv,
    init_s, init_r, ss_s, ss_r, p_s, p_r, x_s, x_r, g_s, g_r, r_s, r_r, b_s, b_r, o_s, o_r, local_sem,
):
    tokens, rows, block, width, half = sizes
    ctx, chan = lax.axis_index("ctx"), lax.axis_index("chan")
    n_ctx, n_chan = 4, 4
    side, core = ctx // 2, ctx % 2
    partner = {"ctx": side * 2 + (1 - core)}
    across = {"ctx": (1 - side) * 2 + core}
    diagonal = {"ctx": (1 - side) * 2 + (1 - core)}
    relations = (partner, across, diagonal)
    last = n_chan - 1
    place = (chan, last - chan)
    onward = ({"chan": jnp.minimum(chan + 1, last)}, {"chan": jnp.maximum(chan - 1, 0)})
    back = (onward[1], onward[0])

    def remote(source, target, send, recv, device):
        return pltpu.make_async_remote_copy(
            src_ref=source, dst_ref=target, send_sem=send, recv_sem=recv,
            device_id=device, device_id_type=pl.DeviceIdType.MESH,
        )

    barrier = pltpu.get_barrier_semaphore()
    for di in range(n_ctx):
        for dk in range(n_chan):
            if di or dk:
                pl.semaphore_signal(
                    barrier, inc=1,
                    device_id={"ctx": (ctx + di) % n_ctx, "chan": (chan + dk) % n_chan},
                    device_id_type=pl.DeviceIdType.MESH,
                )
    pl.semaphore_wait(barrier, n_ctx * n_chan - 1)

    block_rows = tokens // n_ctx
    mine = pl.ds(pl.multiple_of(ctx * block_rows, block_rows), block_rows)

    def init_copy(kappa):
        return remote(stream, h.at[mine, :], init_s.at[kappa], init_r.at[ctx], {"ctx": chan, "chan": kappa})

    def init_wait(source):
        there = pl.ds(source * block_rows, block_rows)
        return remote(stream, h.at[there, :], init_s.at[0], init_r.at[source], {"ctx": chan, "chan": 0})

    corner = ctx == chan
    for kappa in range(n_chan):
        @pl.when(jnp.logical_not(corner & (chan == kappa)))
        def _():
            init_copy(kappa).start()

    @pl.when(corner)
    def _():
        keep = pltpu.make_async_copy(stream, h.at[mine, :], local_sem)
        keep.start()
        keep.wait()

    mixed[pl.ds(0, PAD), :] = jnp.zeros((PAD, LANES), F32)
    for source in range(n_ctx):
        @pl.when(jnp.logical_not(corner & (ctx == source)))
        def _():
            init_wait(source).wait_recv()
    for kappa in range(n_chan):
        @pl.when(jnp.logical_not(corner & (chan == kappa)))
        def _():
            init_copy(kappa).wait_send()

    def span(t):
        return pl.ds(pl.multiple_of(t * rows, rows), rows)

    def ss_copy(rel, t):
        return remote(ss_own.at[t], ss_recv.at[rel, t], ss_s.at[rel, t], ss_r.at[rel, t], relations[rel])

    def p_copy(slot, t):
        return remote(p_send.at[slot, t], p_recv.at[slot, t], p_s.at[slot, t], p_r.at[slot, t], partner)

    def x_copy(t):
        return remote(x_send.at[t], x_recv.at[t], x_s.at[t], x_r.at[t], across)

    def lanes(index):
        return pl.ds(pl.multiple_of(index * LANES, LANES), LANES)

    def g_copy(kind, t, sending=True):
        owner = (1 - side) * 2 + core if kind == 2 else ctx
        if not sending:
            owner = (across["ctx"], partner["ctx"], diagonal["ctx"])[kind]
        ref = gat.at[span(t), lanes(owner)]
        return remote(ref, ref, g_s.at[kind, t], g_r.at[kind, t], across if kind == 0 else partner)

    def r_copy(d, t):
        return remote(r_send.at[d, t], r_recv.at[d, t], r_s.at[d, t], r_r.at[d, t], onward[d])

    def b_copy(d, t):
        ref = h.at[span(t), pl.ds(d * half, half)]
        return remote(ref, ref, b_s.at[d, t], b_r.at[d, t], back[d])

    def arrive(t):
        for d in range(2):
            @pl.when(place[d] == 0)
            def _():
                b_copy(d, t).wait_recv()

    def each(count, body):
        def wrapped(t, carry):
            body(t)
            return carry
        lax.fori_loop(0, count, wrapped, 0)

    def project(section, t, index):
        columns = lanes(index)
        weights = jnp.concatenate([w_in[section, j, :, columns] for j in range(3)], 1)
        return jnp.dot(h[span(t), :], weights, preferred_element_type=F32)

    def enter(section, t):
        p_send[0, t] = project(section, t, diagonal["ctx"]).astype(BF)
        p_copy(0, t).start()
        p_send[1, t] = project(section, t, partner["ctx"]).astype(BF)
        p_copy(1, t).start()
        wide = h[span(t), :].astype(F32)
        squares = (wide * wide).astype(BF)
        ss_own[t] = lax.dot_general(
            jnp.ones((8, squares.shape[1]), BF), squares, (((1,), (1,)), ((), ())), preferred_element_type=F32
        )
        for rel in range(3):
            ss_copy(rel, t).start()

    def cross(section, t):
        passing = project(section, t, across["ctx"])
        p_copy(0, t).wait_recv()
        x_send[t] = (passing + p_recv[0, t].astype(F32)).astype(BF)
        x_copy(t).start()
        own[t] = project(section, t, ctx)

    def entering(s, u):
        section = plan[s]

        @pl.when((u >= 0) & (u < CHUNKS))
        def _():
            @pl.when(s > 0)
            def _():
                arrive(u)

            enter(section, u)

        @pl.when((u > 0) & (u <= CHUNKS))
        def _():
            cross(section, u - 1)

    def step(s, carry):
        section = plan[s]

        def mix(t):
            for rel in range(3):
                ss_copy(rel, t).wait_recv()
            p_copy(1, t).wait_recv()
            x_copy(t).wait_recv()
            total = ss_own[t] + ss_recv[0, t] + ss_recv[1, t] + ss_recv[2, t]
            scale = lax.rsqrt(total * (1.0 / width) + 1e-05)
            scale = jnp.transpose(scale)[:, :1]
            parts = (own[t] + p_recv[1, t].astype(F32) + x_recv[t].astype(F32)) * scale
            query = parts[:, :LANES].astype(BF).astype(F32)
            product = parts[:, LANES:2 * LANES] * parts[:, 2 * LANES:]
            mixed[pl.ds(pl.multiple_of(PAD + t * rows, rows), rows), :] = product.astype(BF).astype(F32)

            def tap_block(jj, total):
                start = pl.multiple_of(PAD + t * rows - 8 * jj - 8, 8)
                window = mixed[pl.ds(start, rows + 8), :]
                weights = taps[section, jj]
                for c in range(8):
                    total = total + weights[c:c + 1, :] * window[8 - c:8 - c + rows, :]
                return total

            filtered = lax.fori_loop(0, taps.shape[1], tap_block, jnp.zeros((rows, LANES), F32))
            gat[span(t), lanes(ctx)] = (query * filtered).astype(BF)
            g_copy(0, t).start()
            g_copy(1, t).start()

        def emit(t):
            g_copy(0, t, False).wait_recv()
            g_copy(2, t).start()
            g_copy(1, t, False).wait_recv()

        def emit_dot(t):
            g_copy(2, t, False).wait_recv()
            gated = gat[span(t), :]
            for d in range(2):
                acc[d, t] = lax.dot_general(
                    gated, w_out[section, d], (((1,), (1,)), ((), ())), preferred_element_type=F32
                )

                @pl.when(place[d] == 0)
                def _():
                    r_send[d, t] = acc[d, t].astype(BF)
                    r_copy(d, t).start()

            @pl.when(s > 0)
            def _():
                for d in range(2):
                    @pl.when((place[d] < last) & (place[d] > 0))
                    def _():
                        b_copy(d, t).wait_send()

                    @pl.when(place[d] == last)
                    def _():
                        b_copy(d, t).wait_send()

        def filtering(u):
            for lag, body in ((0, mix), (2, emit), (4, emit_dot)):
                @pl.when((u >= lag) & (u < CHUNKS + lag))
                def _():
                    body(u - lag)

        each(CHUNKS + 4, filtering)

        def settle(t):
            for slot in range(2):
                p_copy(slot, t).wait_send()
            for rel in range(3):
                ss_copy(rel, t).wait_send()
            x_copy(t).wait_send()
            for kind in range(3):
                g_copy(kind, t).wait_send()

        each(CHUNKS, settle)

        def chain(u):
            for d in range(2):
                t = u - (place[d] - 1) * SKEW
                inside = (t >= 0) & (t < CHUNKS)

                @pl.when(inside & (place[d] > 0) & (place[d] < last))
                def _():
                    r_copy(d, t).wait_recv()
                    r_send[d, t] = (acc[d, t] + r_recv[d, t].astype(F32)).astype(BF)
                    r_copy(d, t).start()

                @pl.when(inside & (place[d] == last))
                def _():
                    r_copy(d, t).wait_recv()
                    update = acc[d, t] + r_recv[d, t].astype(F32)
                    columns = pl.ds(d * half, half)
                    h[span(t), columns] = (h[span(t), columns].astype(F32) + update).astype(BF)
                    b_copy(d, t).start()

            for d in range(2):
                t = u - (2 + last - place[d]) * SKEW
                inside = (t >= 0) & (t < CHUNKS)

                @pl.when(inside & (place[d] > 0) & (place[d] < last))
                def _():
                    b_copy(d, t).wait_recv()
                    b_copy(d, t).start()

            @pl.when(s + 1 < STEPS)
            def _():
                entering(s + 1, u - ENTRY)

        each(jnp.where(s + 1 < STEPS, CHUNKS + 1 + ENTRY, CHUNKS + (2 * last - 2) * SKEW), chain)


        def settle_chain(t):
            for d in range(2):
                @pl.when(place[d] < last)
                def _():
                    r_copy(d, t).wait_send()

        each(CHUNKS, settle_chain)
        return carry

    each(CHUNKS + 1, partial(entering, 0))
    lax.fori_loop(0, STEPS, step, 0)
    each(CHUNKS, arrive)

    def finish(t):
        for d in range(2):
            @pl.when(place[d] > 0)
            def _():
                b_copy(d, t).wait_send()

    each(CHUNKS, finish)

    def out_copy(target):
        there = pl.ds(target * block_rows, block_rows)
        return remote(h.at[there, :], out, o_s.at[target], o_r, {"ctx": target})

    @pl.when(corner)
    def _():
        for target in range(n_ctx):
            @pl.when(ctx != target)
            def _():
                out_copy(target).start()
        keep = pltpu.make_async_copy(h.at[mine, :], out, local_sem)
        keep.start()
        keep.wait()
        for target in range(n_ctx):
            @pl.when(ctx != target)
            def _():
                out_copy(target).wait_send()

    @pl.when(jnp.logical_not(corner))
    def _():
        out_copy(0).wait_recv()


def stationary(stream, in_weights, out_weights, short_taps, medium_taps, plan):
    n_ctx = lax.axis_size("ctx")
    n_chan = lax.axis_size("chan")
    ctx = lax.axis_index("ctx")
    features, channels = in_weights.shape[1], in_weights.shape[3]
    tokens = stream.shape[0] * n_ctx
    rows = tokens // CHUNKS
    half = features // 2
    block = 3 * LANES
    reach = medium_taps.shape[0]
    w_in = in_weights.transpose(0, 2, 1, 3)
    w_out = out_weights.reshape(2, 2, half, channels)
    taps = jnp.stack([section_taps(section, short_taps, medium_taps) for section in range(2)])
    taps = lax.dynamic_slice_in_dim(taps, ctx * LANES, LANES, 2).astype(F32)
    taps = taps.reshape(2, reach // 8, 8, LANES)
    vmem = pl.BlockSpec(memory_space=pltpu.VMEM)
    dma = pltpu.SemaphoreType.DMA
    scratch = [
        pltpu.VMEM((tokens, features), BF),
        pltpu.VMEM((2, CHUNKS, rows, block), BF),
        pltpu.VMEM((2, CHUNKS, rows, block), BF),
        pltpu.VMEM((CHUNKS, rows, block), BF),
        pltpu.VMEM((CHUNKS, rows, block), BF),
        pltpu.VMEM((CHUNKS, rows, block), F32),
        pltpu.VMEM((CHUNKS, 8, rows), F32),
        pltpu.VMEM((3, CHUNKS, 8, rows), F32),
        pltpu.VMEM((PAD + tokens, LANES), F32),
        pltpu.VMEM((8, LANES), F32),
        pltpu.VMEM((tokens, channels), BF),
        pltpu.VMEM((2, CHUNKS, rows, half), F32),
        pltpu.VMEM((2, CHUNKS, rows, half), BF),
        pltpu.VMEM((2, CHUNKS, rows, half), BF),
        dma((n_chan,)), dma((n_ctx,)),
        dma((3, CHUNKS)), dma((3, CHUNKS)),
        dma((2, CHUNKS)), dma((2, CHUNKS)),
        dma((CHUNKS,)), dma((CHUNKS,)),
        dma((3, CHUNKS)), dma((3, CHUNKS)),
        dma((2, CHUNKS)), dma((2, CHUNKS)),
        dma((2, CHUNKS)), dma((2, CHUNKS)),
        dma((n_ctx,)), dma(()), dma(()),
    ]
    sizes = (tokens, rows, block, features * n_ctx, half)
    return pl.pallas_call(
        partial(stationary_kernel, sizes),
        out_shape=jax.ShapeDtypeStruct(stream.shape, stream.dtype),
        in_specs=[pl.BlockSpec(memory_space=pltpu.SMEM)] + [vmem] * 4,
        out_specs=vmem,
        scratch_shapes=scratch,
        compiler_params=pltpu.CompilerParams(
            collective_id=0, has_side_effects=True, vmem_limit_bytes=60 * 1024 * 1024
        ),
    )(plan, stream, w_in, w_out, taps)


def fits(mesh, stream, in_weights, medium_taps):
    n_ctx, n_chan = mesh.shape["ctx"], mesh.shape["chan"]
    tokens = stream.shape[0] // mesh.shape["groups"]
    channels = in_weights.shape[3] // n_chan
    return (
        n_ctx == 4 and n_chan == 4 and channels == n_ctx * LANES
        and stream.shape[1] // n_chan == in_weights.shape[1] // n_ctx
        and tokens % (CHUNKS * PAD) == 0 and medium_taps.shape[0] <= PAD
    )


def solution(mesh):
    def run(stream, in_weights, out_weights, short_taps, medium_taps, plan):
        body = stationary if fits(mesh, stream, in_weights, medium_taps) else shards
        return jax.shard_map(
            body,
            mesh=mesh,
            in_specs=(
                P(("groups", "ctx"), "chan"),
                P(None, "ctx", None, "chan"),
                P(None, "ctx", "chan"),
                P(None, "chan"),
                P(None, "chan"),
                P(),
            ),
            out_specs=P(("groups", "ctx"), "chan"),
            check_vma=False,
        )(stream, in_weights, out_weights, short_taps, medium_taps, plan)

    return run
```
